512 devices in a mesh: section: 16 (over z, core), tensor: 32 (over y, x).
Axes of the slice: x: 4, y: 8, z: 8, core: 2. Of those that a mesh axis runs over, the one named last changes fastest.
Arguments:
- acts_prev: bfloat16 [8192, 8192], P('section', 'tensor'), may hold values from -6 to 6
- embedded: bfloat16 [512, 8192], P(None, 'tensor'), may hold values from -6 to 6
- grads_next: bfloat16 [8192, 8192], P('section', 'tensor'), may hold values from -1.5 to 1.5
- loss_grad: bfloat16 [512, 8192], P(None, 'tensor'), may hold values from -1.5 to 1.5
- up_weight: bfloat16 [16, 2, 256, 32768], P('section', None, None, 'tensor'), may hold values from -0.25 to 0.25
- down_weight: bfloat16 [16, 2, 32768, 256], P('section', None, 'tensor'), may hold values from -0.125 to 0.125
Outputs:
- mixed: bfloat16 [8192, 8192], P('section', 'tensor')
- input_grads: bfloat16 [8192, 8192], P('section', 'tensor')
- up_grad: bfloat16 [16, 2, 256, 32768], P('section', None, None, 'tensor')
- down_grad: bfloat16 [16, 2, 32768, 256], P('section', None, 'tensor')
The draws below stay inside these ranges and needn't reach their ends.
All inputs are finite; a program needn't handle non-finite values.
Results may differ from the reference program's by a relative error of at most 0.005.
Values may be sent and summed in bfloat16 or wider, within the bound.
A program may use at most 64 MiB of HBM per device.

```python
import jax
import jax.numpy as jnp
from jax import lax

D = 8192
H = 32768
BLK = 256
LEVELS = 1
TOK = 512
DBLOCKS = 32
HBLOCKS = 128
EXPAND = 4
N_SECTION = 16
N_TENSOR = 32


def shard_levels(own_key, shape, pieces, least, largest):
    loudness = 1.0
    for axis_at, parts in pieces:
        heights = jax.random.uniform(jax.random.fold_in(jax.random.fold_in(own_key, 6), axis_at), (parts,), jnp.float32, least / len(pieces), largest / len(pieces))
        loudness = loudness * jnp.repeat(jnp.exp(heights), shape[axis_at] // parts).reshape((-1,) + (1,) * (len(shape) - 1 - axis_at))
    return loudness


def centred(stream_key, dims, scale, limit, pieces=(), kind=jnp.bfloat16):
    drawn = scale * jax.random.normal(stream_key, dims, jnp.float32)
    if pieces:
        drawn = drawn * shard_levels(stream_key, dims, pieces, -0.22, 0.18)
    return jnp.clip(drawn, -limit, limit).astype(kind)


def setup_inputs(seed: int = 0) -> dict:
    streams_of = jax.random.split(jax.random.key(seed), 7)
    acts_prev = centred(streams_of[0], (N_SECTION * TOK, D), 1.0, 6.0, ((0, 16), (1, 32)))
    embedded = centred(streams_of[1], (TOK, D), 1.0, 6.0, ((1, 32),))
    grads_next = centred(streams_of[2], (N_SECTION * TOK, D), 0.25, 1.5, ((0, 16), (1, 32)))
    loss_grad = centred(streams_of[3], (TOK, D), 0.25, 1.5, ((1, 32),))
    up_weight = centred(streams_of[4], (N_SECTION, LEVELS + 1, BLK, H), ((LEVELS + 1) * BLK) ** -0.5, 0.25, ((0, 16), (3, 32)))
    down_weight = centred(streams_of[5], (N_SECTION, LEVELS + 1, H, BLK), ((LEVELS + 1) * EXPAND * BLK) ** -0.5, 0.125, ((0, 16), (2, 32)))
    return {"acts_prev": acts_prev, "embedded": embedded, "grads_next": grads_next, "loss_grad": loss_grad, "up_weight": up_weight, "down_weight": down_weight}


def gelu_tanh(values):
    return jax.nn.gelu(values, approximate=True)

def reference(acts_prev, embedded, grads_next, loss_grad, up_weight, down_weight):
    factors = LEVELS + 1
    previous = acts_prev.reshape(N_SECTION, TOK, D)
    section_inputs = jnp.concatenate([embedded[None], previous[:-1]], axis=0)
    following = grads_next.reshape(N_SECTION, TOK, D)
    section_grads = jnp.concatenate([following[1:], loss_grad[None]], axis=0)
    per_device = DBLOCKS // N_TENSOR
    block_ids = jnp.arange(DBLOCKS, dtype=jnp.int32)
    tables = [block_ids]
    for level_idx in range(LEVELS):
        far = N_TENSOR >> LEVELS - level_idx
        tables.append((jnp.bitwise_xor(block_ids // per_device, far) * per_device + block_ids % per_device).astype(jnp.int32))
    anchor = (jnp.arange(HBLOCKS, dtype=jnp.int32) // EXPAND).astype(jnp.int32)

    def section_layer(operands):
        inputs, cotangent, up_section, down_section = operands
        inputs_f = inputs.astype(jnp.float32).reshape(TOK, DBLOCKS, BLK)
        grads_f = cotangent.astype(jnp.float32).reshape(TOK, DBLOCKS, BLK)
        up_f = up_section.astype(jnp.float32).reshape(factors, BLK, HBLOCKS, BLK)
        down_f = down_section.astype(jnp.float32).reshape(factors, HBLOCKS, BLK, BLK)
        seen_x = [inputs_f[:, table][:, anchor] for table in tables]
        seen_g = [grads_f[:, table][:, anchor] for table in tables]
        pre = jnp.zeros((TOK, HBLOCKS, BLK), jnp.float32)
        for factor in range(factors):
            pre = pre + jnp.einsum('tjp,pjq->tjq', seen_x[factor], up_f[factor])
        hidden = gelu_tanh(pre).astype(jnp.bfloat16)
        hidden_f = hidden.astype(jnp.float32)
        branch = jnp.zeros((TOK, DBLOCKS, BLK), jnp.float32)
        for factor in range(factors):
            part = jnp.einsum('tjp,jpq->tjq', hidden_f, down_f[factor]).reshape(TOK, DBLOCKS, EXPAND, BLK).sum(axis=2)
            if factor > 0:
                part = lax.optimization_barrier(part.astype(jnp.bfloat16)).astype(jnp.float32)[:, tables[factor]]
            branch = branch + part
        mixed = (inputs_f + branch).reshape(TOK, D).astype(jnp.bfloat16)
        grad_hidden = jnp.zeros((TOK, HBLOCKS, BLK), jnp.float32)
        down_grads = []
        for factor in range(factors):
            grad_hidden = grad_hidden + jnp.einsum('tjq,jpq->tjp', seen_g[factor], down_f[factor])
            down_grads.append(jnp.einsum('tjp,tjq->jpq', hidden_f, seen_g[factor]))
        down_grad = jnp.stack(down_grads).reshape(factors, H, BLK).astype(jnp.bfloat16)
        pullback = jax.vjp(gelu_tanh, pre)[1]
        grad_pre = pullback(grad_hidden)[0].astype(jnp.bfloat16).astype(jnp.float32)
        up_grads = []
        back_sum = grads_f
        for factor in range(factors):
            up_grads.append(jnp.einsum('tjp,tjq->pjq', seen_x[factor], grad_pre))
            back = jnp.einsum('tjq,pjq->tjp', grad_pre, up_f[factor]).reshape(TOK, DBLOCKS, EXPAND, BLK).sum(axis=2)
            if factor > 0:
                back = lax.optimization_barrier(back.astype(jnp.bfloat16)).astype(jnp.float32)[:, tables[factor]]
            back_sum = back_sum + back
        up_grad = jnp.stack(up_grads).reshape(factors, BLK, H).astype(jnp.bfloat16)
        input_grads = back_sum.reshape(TOK, D).astype(jnp.bfloat16)
        return (mixed, input_grads, up_grad, down_grad)
    mixed, input_grads, up_grad, down_grad = lax.map(section_layer, (section_inputs, section_grads, up_weight, down_weight))
    return (mixed.reshape(N_SECTION * TOK, D), input_grads.reshape(N_SECTION * TOK, D), up_grad, down_grad)
```

```python
import functools

import jax
import jax.numpy as jnp
from jax import lax
from jax.experimental import pallas as pl
from jax.experimental.pallas import tpu as pltpu
from jax.sharding import PartitionSpec as P

MESH = pl.DeviceIdType.MESH
F32 = jnp.float32
BF16 = jnp.bfloat16
CHUNKS = 4
ROOT = 0.7978845608028654
CUBIC = 0.044715


def dot(a, b):
    return jnp.dot(a, b, preferred_element_type=F32)


def dot_nt(a, b):
    return lax.dot_general(a, b, (((1,), (1,)), ((), ())), preferred_element_type=F32)


def dot_tn(a, b):
    return lax.dot_general(a, b, (((0,), (0,)), ((), ())), preferred_element_type=F32)


def kernel(
    sections, far, expand,
    acts, emb, grads, loss, up, down,
    mixed, input_grads, up_grad, down_grad,
    x_own, x_far, g_own, g_far, u, v, hid, gpre, out_own, back_own,
    out_send, back_send, out_got, back_got, mixed_v, ingrad_v, upg_v, downg_v,
    send_sem, recv_sem, load_sem, store_sem, mix_sem,
):
    chunks, rows, width = x_own.shape
    section, tensor = lax.axis_index("section"), lax.axis_index("tensor")
    partner = tensor + far - 2 * far * (lax.rem(tensor // far, 2))
    first, last = section == 0, section == sections - 1

    def at(step, place):
        return {"section": section + step, "tensor": place}

    load_u = pltpu.make_async_copy(up, u, load_sem.at[0])
    load_v = pltpu.make_async_copy(down, v, load_sem.at[1])
    load_u.start()
    load_v.start()

    barrier = pltpu.get_barrier_semaphore()

    def greet(step, place):
        pl.semaphore_signal(barrier, inc=1, device_id=at(step, place), device_id_type=MESH)

    greet(0, partner)

    @pl.when(jnp.logical_not(last))
    def _():
        greet(1, partner)
        greet(1, tensor)

    @pl.when(jnp.logical_not(first))
    def _():
        greet(-1, partner)
        greet(-1, tensor)

    edge = jnp.logical_or(first, last)

    @pl.when(edge)
    def _():
        pl.semaphore_wait(barrier, 3)

    @pl.when(jnp.logical_not(edge))
    def _():
        pl.semaphore_wait(barrier, 5)

    def part(ref, c):
        return ref.at[pl.ds(pl.multiple_of(c * rows, rows), rows)]

    def copy(source, target, c, send, recv, step, place):
        return pltpu.make_async_remote_copy(
            src_ref=source,
            dst_ref=target.at[c],
            send_sem=send_sem.at[send, c],
            recv_sem=recv_sem.at[recv, c],
            device_id=at(step, place),
            device_id_type=MESH,
        )

    def acts_far(c):
        return copy(part(acts, c), x_far, c, 0, 0, 1, partner)

    def grads_far(c):
        return copy(part(grads, c), g_far, c, 1, 1, -1, partner)

    def acts_near(c):
        return copy(part(acts, c), x_own, c, 2, 2, 1, tensor)

    def grads_near(c):
        return copy(part(grads, c), g_own, c, 3, 3, -1, tensor)

    def emb_far(c):
        return copy(part(emb, c), x_far, c, 4, 0, 0, partner)

    def loss_far(c):
        return copy(part(loss, c), g_far, c, 4, 1, 0, partner)

    def emb_near(c):
        return pltpu.make_async_copy(part(emb, c), x_own.at[c], recv_sem.at[2, c])

    def loss_near(c):
        return pltpu.make_async_copy(part(loss, c), g_own.at[c], recv_sem.at[3, c])

    def out_copy(c):
        return copy(out_send.at[c], out_got, c, 5, 4, 0, partner)

    def back_copy(c):
        return copy(back_send.at[c], back_got, c, 6, 5, 0, partner)

    def start(c, carry):
        @pl.when(jnp.logical_not(last))
        def _():
            acts_far(c).start()
            acts_near(c).start()

        @pl.when(first)
        def _():
            emb_far(c).start()
            emb_near(c).start()

        @pl.when(jnp.logical_not(first))
        def _():
            grads_far(c).start()
            grads_near(c).start()

        @pl.when(last)
        def _():
            loss_far(c).start()
            loss_near(c).start()

        return carry

    lax.fori_loop(0, chunks, start, 0)
    load_u.wait()
    load_v.wait()

    def compute(c, carry):
        acts_far(c).wait_recv()
        acts_near(c).wait_recv()
        here = pl.ds(pl.multiple_of(c * rows, rows), rows)
        xo, xf = x_own[c], x_far[c]
        slopes = []
        out0 = xo.astype(F32)
        out1 = jnp.zeros((rows, width), F32)
        for j in range(expand):
            block = slice(j * width, (j + 1) * width)
            pre = dot(xo, u[0, :, block]) + dot(xf, u[1, :, block])
            square = pre * pre
            t = jnp.tanh(ROOT * (pre + CUBIC * (square * pre)))
            half = 0.5 * (1.0 + t)
            slopes.append(
                half + 0.5 * pre * (1.0 - t * t) * (ROOT * (1.0 + 3.0 * CUBIC * square))
            )
            h = (pre * half).astype(BF16)
            hid[here, block] = h
            out1 = out1 + dot(h, v[1, block, :])
            out0 = out0 + dot(h, v[0, block, :])
        out_send[c] = out1.astype(BF16)
        out_copy(c).start()
        out_own[c] = out0
        grads_far(c).wait_recv()
        grads_near(c).wait_recv()
        go, gf = g_own[c], g_far[c]
        back0 = go.astype(F32)
        back1 = jnp.zeros((rows, width), F32)
        for j in range(expand):
            block = slice(j * width, (j + 1) * width)
            gh = dot_nt(go, v[0, block, :]) + dot_nt(gf, v[1, block, :])
            gp = (gh * slopes[j]).astype(BF16)
            gpre[here, block] = gp
            back1 = back1 + dot_nt(gp, u[1, :, block])
            back0 = back0 + dot_nt(gp, u[0, :, block])
        back_send[c] = back1.astype(BF16)
        back_copy(c).start()
        back_own[c] = back0
        return carry

    lax.fori_loop(0, chunks, compute, 0)

    flat = (chunks * rows, width)
    for k, (xk, gk) in enumerate(((x_own, g_own), (x_far, g_far))):
        xs, gs = xk[...].reshape(flat), gk[...].reshape(flat)
        for j in range(expand):
            block = slice(j * width, (j + 1) * width)
            upg_v[k, :, block] = dot_tn(xs, gpre[:, block]).astype(BF16)
            downg_v[k, block, :] = dot_tn(hid[:, block], gs).astype(BF16)
    store_u = pltpu.make_async_copy(upg_v, up_grad, store_sem.at[0])
    store_d = pltpu.make_async_copy(downg_v, down_grad, store_sem.at[1])
    store_u.start()
    store_d.start()

    def store_mixed(c):
        return pltpu.make_async_copy(mixed_v.at[c], part(mixed, c), mix_sem.at[0, c])

    def store_ingrad(c):
        return pltpu.make_async_copy(ingrad_v.at[c], part(input_grads, c), mix_sem.at[1, c])

    def finish(c, carry):
        out_copy(c).wait_recv()
        mixed_v[c] = (out_own[c] + out_got[c].astype(F32)).astype(BF16)
        store_mixed(c).start()
        back_copy(c).wait_recv()
        ingrad_v[c] = (back_own[c] + back_got[c].astype(F32)).astype(BF16)
        store_ingrad(c).start()
        return carry

    lax.fori_loop(0, chunks, finish, 0)

    def drain(c, carry):
        out_copy(c).wait_send()
        back_copy(c).wait_send()

        @pl.when(jnp.logical_not(last))
        def _():
            acts_far(c).wait_send()
            acts_near(c).wait_send()

        @pl.when(first)
        def _():
            emb_far(c).wait_send()

        @pl.when(jnp.logical_not(first))
        def _():
            grads_far(c).wait_send()
            grads_near(c).wait_send()

        @pl.when(last)
        def _():
            loss_far(c).wait_send()

        store_mixed(c).wait()
        store_ingrad(c).wait()
        return carry

    lax.fori_loop(0, chunks, drain, 0)
    store_u.wait()
    store_d.wait()


def on_device(acts_prev, embedded, grads_next, loss_grad, up_weight, down_weight):
    sections, tensors = lax.axis_size("section"), lax.axis_size("tensor")
    tokens, width = acts_prev.shape
    up_local, down_local = up_weight[0], down_weight[0]
    factors, _, hidden = up_local.shape
    chunks, rows = CHUNKS, tokens // CHUNKS
    blocks = (chunks, rows, width)
    anywhere = pl.BlockSpec(memory_space=pl.ANY)

    def in_hbm(value):
        return pltpu.with_memory_space_constraint(value, pltpu.HBM)

    mixed, input_grads, up_grad, down_grad = pl.pallas_call(
        functools.partial(kernel, sections, tensors // 2, hidden // width),
        name="relay_layer",
        out_shape=(
            jax.ShapeDtypeStruct((tokens, width), BF16),
            jax.ShapeDtypeStruct((tokens, width), BF16),
            jax.ShapeDtypeStruct(up_local.shape, BF16),
            jax.ShapeDtypeStruct(down_local.shape, BF16),
        ),
        in_specs=[anywhere] * 6,
        out_specs=[anywhere] * 4,
        scratch_shapes=[
            pltpu.VMEM(blocks, BF16),
            pltpu.VMEM(blocks, BF16),
            pltpu.VMEM(blocks, BF16),
            pltpu.VMEM(blocks, BF16),
            pltpu.VMEM(up_local.shape, BF16),
            pltpu.VMEM(down_local.shape, BF16),
            pltpu.VMEM((tokens, hidden), BF16),
            pltpu.VMEM((tokens, hidden), BF16),
            pltpu.VMEM(blocks, F32),
            pltpu.VMEM(blocks, F32),
            pltpu.VMEM(blocks, BF16),
            pltpu.VMEM(blocks, BF16),
            pltpu.VMEM(blocks, BF16),
            pltpu.VMEM(blocks, BF16),
            pltpu.VMEM(blocks, BF16),
            pltpu.VMEM(blocks, BF16),
            pltpu.VMEM(up_local.shape, BF16),
            pltpu.VMEM(down_local.shape, BF16),
            pltpu.SemaphoreType.DMA((7, chunks)),
            pltpu.SemaphoreType.DMA((6, chunks)),
            pltpu.SemaphoreType.DMA((2,)),
            pltpu.SemaphoreType.DMA((2,)),
            pltpu.SemaphoreType.DMA((2, chunks)),
        ],
        compiler_params=pltpu.CompilerParams(
            collective_id=0, has_side_effects=True, vmem_limit_bytes=48 << 20
        ),
    )(*map(in_hbm, (acts_prev, embedded, grads_next, loss_grad, up_local, down_local)))
    return (mixed, input_grads, up_grad[None], down_grad[None])


def solution(mesh):
    in_specs = (
        P("section", "tensor"),
        P(None, "tensor"),
        P("section", "tensor"),
        P(None, "tensor"),
        P("section", None, None, "tensor"),
        P("section", None, "tensor", None),
    )
    out_specs = (
        P("section", "tensor"),
        P("section", "tensor"),
        P("section", None, None, "tensor"),
        P("section", None, "tensor", None),
    )
    return jax.shard_map(
        on_device, mesh=mesh, in_specs=in_specs, out_specs=out_specs, check_vma=False
    )
```

```python
import functools

import jax
import jax.numpy as jnp
from jax import lax
from jax.experimental import pallas as pl
from jax.experimental.pallas import tpu as pltpu
from jax.sharding import PartitionSpec as P

MESH = pl.DeviceIdType.MESH
F32 = jnp.float32
BF16 = jnp.bfloat16
CHUNKS = 4
ROOT = 0.7978845608028654
CUBIC = 0.044715


def dot(a, b):
    return jnp.dot(a, b, preferred_element_type=F32)


def dot_nt(a, b):
    return lax.dot_general(a, b, (((1,), (1,)), ((), ())), preferred_element_type=F32)


def dot_tn(a, b):
    return lax.dot_general(a, b, (((0,), (0,)), ((), ())), preferred_element_type=F32)


def kernel(
    sections, far, expand,
    acts, emb, grads, loss, up, down,
    mixed, input_grads, up_grad, down_grad,
    x_own, x_far, g_own, g_far, u, v, hid, gpre, out_own, back_own,
    out_send, back_send, out_got, back_got,
    send_sem, recv_sem, load_sem, ready,
):
    chunks, rows, width = x_own.shape
    section, tensor = lax.axis_index("section"), lax.axis_index("tensor")
    partner = tensor + far - 2 * far * (lax.rem(tensor // far, 2))
    first, last = section == 0, section == sections - 1

    def at(step, place):
        return {"section": section + step, "tensor": place}

    load_u = pltpu.make_async_copy(up, u, load_sem.at[0])
    load_v = pltpu.make_async_copy(down, v, load_sem.at[1])
    load_u.start()
    load_v.start()

    corner = jnp.logical_or(tensor == 0, tensor == far)
    late = jnp.logical_and(first, tensor == 0)
    hears_late = jnp.logical_and(
        jnp.logical_and(section <= 1, corner), jnp.logical_not(late)
    )
    edge = jnp.logical_or(first, last)
    barrier = pltpu.get_barrier_semaphore()

    def tell(semaphore, step, place):
        pl.semaphore_signal(
            semaphore, inc=1, device_id=at(step, place), device_id_type=MESH
        )

    def tell_all(semaphore):
        tell(semaphore, 0, partner)

        @pl.when(jnp.logical_not(last))
        def _():
            tell(semaphore, 1, partner)
            tell(semaphore, 1, tensor)

        @pl.when(jnp.logical_not(first))
        def _():
            tell(semaphore, -1, partner)
            tell(semaphore, -1, tensor)

    def wait_for(peers, when):
        @pl.when(when)
        def _():
            pl.semaphore_wait(barrier, peers)

    pl.when(jnp.logical_not(late))(lambda: tell_all(barrier))
    inner, prompt = jnp.logical_not(edge), jnp.logical_not(hears_late)
    wait_for(5, jnp.logical_and(inner, prompt))
    wait_for(4, jnp.logical_and(inner, hears_late))
    wait_for(3, jnp.logical_and(edge, prompt))
    wait_for(2, jnp.logical_and(edge, hears_late))

    @pl.when(late)
    def _():
        tell(ready, 0, partner)
        tell(ready, 1, partner)
        tell(ready, 1, tensor)

    def part(ref, c):
        return ref.at[pl.ds(pl.multiple_of(c * rows, rows), rows)]

    def copy(source, target, c, send, recv, step, place):
        return pltpu.make_async_remote_copy(
            src_ref=source,
            dst_ref=target.at[c],
            send_sem=send_sem.at[send, c],
            recv_sem=recv_sem.at[recv, c],
            device_id=at(step, place),
            device_id_type=MESH,
        )

    def acts_far(c):
        return copy(part(acts, c), x_far, c, 0, 0, 1, partner)

    def grads_far(c):
        return copy(part(grads, c), g_far, c, 1, 1, -1, partner)

    def acts_near(c):
        return copy(part(acts, c), x_own, c, 2, 2, 1, tensor)

    def grads_near(c):
        return copy(part(grads, c), g_own, c, 3, 3, -1, tensor)

    def emb_far(c):
        return copy(part(emb, c), x_far, c, 4, 0, 0, partner)

    def loss_far(c):
        return copy(part(loss, c), g_far, c, 4, 1, 0, partner)

    def emb_near(c):
        return pltpu.make_async_copy(part(emb, c), x_own.at[c], recv_sem.at[2, c])

    def loss_near(c):
        return pltpu.make_async_copy(part(loss, c), g_own.at[c], recv_sem.at[3, c])

    def out_copy(c):
        return copy(out_send.at[c], out_got, c, 5, 4, 0, partner)

    def back_copy(c):
        return copy(back_send.at[c], back_got, c, 6, 5, 0, partner)

    def near_late(step, place):
        return jnp.logical_and(section + step == 0, place == 0)

    far_first = jnp.logical_and(first, jnp.logical_not(near_late(0, partner)))
    down_far = jnp.logical_and(jnp.logical_not(first), jnp.logical_not(near_late(-1, partner)))
    down_near = jnp.logical_and(jnp.logical_not(first), jnp.logical_not(near_late(-1, tensor)))

    def start(c, carry):
        @pl.when(jnp.logical_not(last))
        def _():
            acts_far(c).start()
            acts_near(c).start()

        @pl.when(first)
        def _():
            emb_near(c).start()

        pl.when(far_first)(lambda: emb_far(c).start())
        pl.when(down_far)(lambda: grads_far(c).start())
        pl.when(down_near)(lambda: grads_near(c).start())

        @pl.when(last)
        def _():
            loss_far(c).start()
            loss_near(c).start()

        return carry

    def start_late(c, carry):
        pl.when(near_late(0, partner))(lambda: emb_far(c).start())
        pl.when(near_late(-1, partner))(lambda: grads_far(c).start())
        pl.when(near_late(-1, tensor))(lambda: grads_near(c).start())
        return carry

    lax.fori_loop(0, chunks, start, 0)

    @pl.when(hears_late)
    def _():
        pl.semaphore_wait(ready, 1)
        lax.fori_loop(0, chunks, start_late, 0)

    load_u.wait()
    load_v.wait()

    def compute(c, carry):
        acts_far(c).wait_recv()
        acts_near(c).wait_recv()
        here = pl.ds(pl.multiple_of(c * rows, rows), rows)
        xo, xf = x_own[c], x_far[c]
        slopes = []
        out0 = xo.astype(F32)
        out1 = jnp.zeros((rows, width), F32)
        for j in range(expand):
            block = slice(j * width, (j + 1) * width)
            pre = dot(xo, u[0, :, block]) + dot(xf, u[1, :, block])
            square = pre * pre
            t = jnp.tanh(ROOT * (pre + CUBIC * (square * pre)))
            half = 0.5 * (1.0 + t)
            slopes.append(
                half + 0.5 * pre * (1.0 - t * t) * (ROOT * (1.0 + 3.0 * CUBIC * square))
            )
            h = (pre * half).astype(BF16)
            hid[here, block] = h
            out1 = out1 + dot(h, v[1, block, :])
            out0 = out0 + dot(h, v[0, block, :])
        out_send[c] = out1.astype(BF16)
        out_copy(c).start()
        out_own[c] = out0
        grads_far(c).wait_recv()
        grads_near(c).wait_recv()
        go, gf = g_own[c], g_far[c]
        back0 = go.astype(F32)
        back1 = jnp.zeros((rows, width), F32)
        for j in range(expand):
            block = slice(j * width, (j + 1) * width)
            gh = dot_nt(go, v[0, block, :]) + dot_nt(gf, v[1, block, :])
            gp = (gh * slopes[j]).astype(BF16)
            gpre[here, block] = gp
            back1 = back1 + dot_nt(gp, u[1, :, block])
            back0 = back0 + dot_nt(gp, u[0, :, block])
        back_send[c] = back1.astype(BF16)
        back_copy(c).start()
        back_own[c] = back0
        return carry

    lax.fori_loop(0, chunks, compute, 0)

    flat = (chunks * rows, width)
    for k, (xk, gk) in enumerate(((x_own, g_own), (x_far, g_far))):
        xs, gs = xk[...].reshape(flat), gk[...].reshape(flat)
        for j in range(expand):
            block = slice(j * width, (j + 1) * width)
            up_grad[k, :, block] = dot_tn(xs, gpre[:, block]).astype(BF16)
            down_grad[k, block, :] = dot_tn(hid[:, block], gs).astype(BF16)
    def finish(c, carry):
        out_copy(c).wait_recv()
        here = pl.ds(pl.multiple_of(c * rows, rows), rows)
        mixed[here] = (out_own[c] + out_got[c].astype(F32)).astype(BF16)
        back_copy(c).wait_recv()
        input_grads[here] = (back_own[c] + back_got[c].astype(F32)).astype(BF16)
        return carry

    lax.fori_loop(0, chunks, finish, 0)

    def drain(c, carry):
        out_copy(c).wait_send()
        back_copy(c).wait_send()

        @pl.when(jnp.logical_not(last))
        def _():
            acts_far(c).wait_send()
            acts_near(c).wait_send()

        @pl.when(first)
        def _():
            emb_far(c).wait_send()

        @pl.when(jnp.logical_not(first))
        def _():
            grads_far(c).wait_send()
            grads_near(c).wait_send()

        @pl.when(last)
        def _():
            loss_far(c).wait_send()

        return carry

    lax.fori_loop(0, chunks, drain, 0)


def flush(*refs):
    done = refs[-1]
    count = done.shape[0]
    copies = [
        pltpu.make_async_copy(refs[i], refs[count + i], done.at[i]) for i in range(count)
    ]
    for copy in copies:
        copy.start()
    for copy in copies:
        copy.wait()


def on_device(acts_prev, embedded, grads_next, loss_grad, up_weight, down_weight):
    sections, tensors = lax.axis_size("section"), lax.axis_size("tensor")
    tokens, width = acts_prev.shape
    up_local, down_local = up_weight[0], down_weight[0]
    factors, _, hidden = up_local.shape
    chunks, rows = CHUNKS, tokens // CHUNKS
    blocks = (chunks, rows, width)
    anywhere = pl.BlockSpec(memory_space=pl.ANY)

    def in_hbm(value):
        return pltpu.with_memory_space_constraint(value, pltpu.HBM)

    shapes = (acts_prev.shape, acts_prev.shape, up_local.shape, down_local.shape)
    results = pl.pallas_call(
        functools.partial(kernel, sections, tensors // 2, hidden // width),
        name="relay_layer",
        out_shape=tuple(pltpu.VMEM(shape, BF16) for shape in shapes),
        in_specs=[anywhere] * 6,
        out_specs=[pl.BlockSpec(memory_space=pltpu.VMEM)] * 4,
        scratch_shapes=[
            pltpu.VMEM(blocks, BF16),
            pltpu.VMEM(blocks, BF16),
            pltpu.VMEM(blocks, BF16),
            pltpu.VMEM(blocks, BF16),
            pltpu.VMEM(up_local.shape, BF16),
            pltpu.VMEM(down_local.shape, BF16),
            pltpu.VMEM((tokens, hidden), BF16),
            pltpu.VMEM((tokens, hidden), BF16),
            pltpu.VMEM(blocks, F32),
            pltpu.VMEM(blocks, F32),
            pltpu.VMEM(blocks, BF16),
            pltpu.VMEM(blocks, BF16),
            pltpu.VMEM(blocks, BF16),
            pltpu.VMEM(blocks, BF16),
            pltpu.SemaphoreType.DMA((7, chunks)),
            pltpu.SemaphoreType.DMA((6, chunks)),
            pltpu.SemaphoreType.DMA((2,)),
            pltpu.SemaphoreType.REGULAR,
        ],
        compiler_params=pltpu.CompilerParams(
            collective_id=0, has_side_effects=True, vmem_limit_bytes=48 << 20
        ),
    )(*map(in_hbm, (acts_prev, embedded, grads_next, loss_grad, up_local, down_local)))
    mixed, input_grads, up_grad, down_grad = pl.pallas_call(
        flush,
        name="flush",
        out_shape=tuple(pltpu.HBM(shape, BF16) for shape in shapes),
        in_specs=[anywhere] * 4,
        out_specs=[anywhere] * 4,
        scratch_shapes=[pltpu.SemaphoreType.DMA((4,))],
        compiler_params=pltpu.CompilerParams(vmem_limit_bytes=1 << 20),
    )(*results)
    return (mixed, input_grads, up_grad[None], down_grad[None])


def solution(mesh):
    in_specs = (
        P("section", "tensor"),
        P(None, "tensor"),
        P("section", "tensor"),
        P(None, "tensor"),
        P("section", None, None, "tensor"),
        P("section", None, "tensor", None),
    )
    out_specs = (
        P("section", "tensor"),
        P("section", "tensor"),
        P("section", None, None, "tensor"),
        P("section", None, "tensor", None),
    )
    return jax.shard_map(
        on_device, mesh=mesh, in_specs=in_specs, out_specs=out_specs, check_vma=False
    )
```

```python
import functools

import jax
import jax.numpy as jnp
from jax import lax
from jax.experimental import pallas as pl
from jax.experimental.pallas import tpu as pltpu
from jax.sharding import PartitionSpec as P

MESH = pl.DeviceIdType.MESH
F32 = jnp.float32
BF16 = jnp.bfloat16
CHUNKS = 2
ROOT = 0.7978845608028654
CUBIC = 0.044715


def dot(a, b):
    return jnp.dot(a, b, preferred_element_type=F32)


def dot_nt(a, b):
    return lax.dot_general(a, b, (((1,), (1,)), ((), ())), preferred_element_type=F32)


def dot_tn(a, b):
    return lax.dot_general(a, b, (((0,), (0,)), ((), ())), preferred_element_type=F32)


def kernel(
    sections, far, expand,
    acts, emb, grads, loss, up, down,
    mixed, input_grads, up_grad, down_grad,
    x_own, x_far, g_own, g_far, u, v, hid, gpre, out_own, back_own,
    out_send, back_send, out_got, back_got,
    send_sem, recv_sem, load_sem, ready, upper_in,
):
    chunks, rows, width = x_own.shape
    section, tensor = lax.axis_index("section"), lax.axis_index("tensor")
    partner = tensor + far - 2 * far * (lax.rem(tensor // far, 2))
    first, last = section == 0, section == sections - 1

    def at(step, place):
        return {"section": section + step, "tensor": place}

    load_u = pltpu.make_async_copy(up, u, load_sem.at[0])
    load_v = pltpu.make_async_copy(down, v, load_sem.at[1])

    corner = jnp.logical_or(tensor == 0, tensor == far)
    late = jnp.logical_and(first, tensor == 0)
    hears_late = jnp.logical_and(
        jnp.logical_and(section <= 1, corner), jnp.logical_not(late)
    )
    barrier = pltpu.get_barrier_semaphore()

    def tell(semaphore, step, place):
        pl.semaphore_signal(
            semaphore, inc=1, device_id=at(step, place), device_id_type=MESH
        )

    even = lax.rem(section, 2) == 0
    odd = jnp.logical_not(even)
    other = 1 - 2 * lax.rem(section, 2)
    has_upper = jnp.logical_and(odd, jnp.logical_not(last))
    has_lower = jnp.logical_and(even, jnp.logical_not(first))

    @pl.when(jnp.logical_not(late))
    def _():
        tell(barrier, 0, partner)
        tell(barrier, other, partner)
        tell(barrier, other, tensor)

        pl.when(has_upper)(lambda: tell(barrier, 1, tensor))

    load_u.start()
    load_v.start()

    def wait_for(peers, when):
        @pl.when(when)
        def _():
            pl.semaphore_wait(barrier, peers)

    wait_for(4, has_lower)
    wait_for(3, jnp.logical_and(jnp.logical_not(has_lower), jnp.logical_not(hears_late)))
    wait_for(2, hears_late)

    @pl.when(late)
    def _():
        tell(ready, 0, partner)
        tell(ready, 1, tensor)

    pl.when(has_lower)(lambda: tell(upper_in, -1, tensor))

    def part(ref, c):
        return ref.at[pl.ds(pl.multiple_of(c * rows, rows), rows)]

    def copy(source, target, c, send, recv, step, place):
        return pltpu.make_async_remote_copy(
            src_ref=source,
            dst_ref=target.at[c],
            send_sem=send_sem.at[send, c],
            recv_sem=recv_sem.at[recv, c],
            device_id=at(step, place),
            device_id_type=MESH,
        )

    def acts_far(c):
        return copy(part(acts, c), x_far, c, 0, 0, 1, partner)

    def grads_far(c):
        return copy(part(grads, c), g_far, c, 1, 1, -1, partner)

    def acts_near(c):
        return copy(part(acts, c), x_own, c, 2, 2, 1, tensor)

    def grads_near(c):
        return copy(part(grads, c), g_own, c, 3, 3, -1, tensor)

    def emb_far(c):
        return copy(part(emb, c), x_far, c, 4, 0, 0, partner)

    def loss_far(c):
        return copy(part(loss, c), g_far, c, 4, 1, 0, partner)

    def pass_acts(c):
        return copy(x_own.at[c], x_far, c, 4, 0, 0, partner)

    def pass_grads(c):
        return copy(g_own.at[c], g_far, c, 4, 1, 0, partner)

    def pass_late(c):
        return copy(g_own.at[c], g_far, c, 1, 1, 0, partner)

    def emb_near(c):
        return pltpu.make_async_copy(part(emb, c), x_own.at[c], recv_sem.at[2, c])

    def loss_near(c):
        return pltpu.make_async_copy(part(loss, c), g_own.at[c], recv_sem.at[3, c])

    def out_copy(c):
        return copy(out_send.at[c], out_got, c, 5, 4, 0, partner)

    def back_copy(c):
        return copy(back_send.at[c], back_got, c, 6, 5, 0, partner)

    def near_late(step, place):
        return jnp.logical_and(section + step == 0, place == 0)

    beside_late, across_late = near_late(0, partner), near_late(-1, partner)
    far_first = jnp.logical_and(first, jnp.logical_not(beside_late))
    odd_far = jnp.logical_and(odd, jnp.logical_not(across_late))
    odd_near = jnp.logical_and(odd, jnp.logical_not(near_late(-1, tensor)))

    def start_far(c, carry):
        pl.when(even)(lambda: acts_far(c).start())
        pl.when(odd_far)(lambda: grads_far(c).start())
        pl.when(far_first)(lambda: emb_far(c).start())
        pl.when(last)(lambda: loss_far(c).start())
        return carry

    def start_near(c, carry):
        pl.when(even)(lambda: acts_near(c).start())
        pl.when(jnp.logical_or(odd_near, has_lower))(lambda: grads_near(c).start())
        pl.when(first)(lambda: emb_near(c).start())
        pl.when(last)(lambda: loss_near(c).start())
        return carry

    def start_upper(c, carry):
        acts_near(c).start()
        return carry

    def start_late(c, carry):
        pl.when(beside_late)(lambda: emb_far(c).start())
        pl.when(near_late(-1, tensor))(lambda: grads_near(c).start())
        return carry

    def pass_on(c, carry):
        acts_near(c).wait_recv()
        grads_near(c).wait_recv()
        pl.when(has_lower)(lambda: pass_acts(c).start())
        pl.when(has_upper)(lambda: pass_grads(c).start())
        pl.when(beside_late)(lambda: pass_late(c).start())
        return carry

    lax.fori_loop(0, chunks, start_near, 0)
    lax.fori_loop(0, chunks, start_far, 0)

    @pl.when(has_upper)
    def _():
        pl.semaphore_wait(upper_in, 1)
        lax.fori_loop(0, chunks, start_upper, 0)

    @pl.when(jnp.logical_and(hears_late, jnp.logical_not(across_late)))
    def _():
        pl.semaphore_wait(ready, 1)
        lax.fori_loop(0, chunks, start_late, 0)

    lax.fori_loop(0, chunks, pass_on, 0)
    load_u.wait()
    load_v.wait()

    def compute(c, carry):
        acts_far(c).wait_recv()
        here = pl.ds(pl.multiple_of(c * rows, rows), rows)
        xo, xf = x_own[c], x_far[c]
        slopes = []
        out0 = xo.astype(F32)
        out1 = jnp.zeros((rows, width), F32)
        for j in range(expand):
            block = slice(j * width, (j + 1) * width)
            pre = dot(xo, u[0, :, block]) + dot(xf, u[1, :, block])
            square = pre * pre
            t = jnp.tanh(ROOT * (pre + CUBIC * (square * pre)))
            half = 0.5 * (1.0 + t)
            slopes.append(
                half + 0.5 * pre * (1.0 - t * t) * (ROOT * (1.0 + 3.0 * CUBIC * square))
            )
            h = (pre * half).astype(BF16)
            hid[here, block] = h
            out1 = out1 + dot(h, v[1, block, :])
            out0 = out0 + dot(h, v[0, block, :])
        out_send[c] = out1.astype(BF16)
        out_copy(c).start()
        out_own[c] = out0
        grads_far(c).wait_recv()
        go, gf = g_own[c], g_far[c]
        back0 = go.astype(F32)
        back1 = jnp.zeros((rows, width), F32)
        for j in range(expand):
            block = slice(j * width, (j + 1) * width)
            gh = dot_nt(go, v[0, block, :]) + dot_nt(gf, v[1, block, :])
            gp = (gh * slopes[j]).astype(BF16)
            gpre[here, block] = gp
            back1 = back1 + dot_nt(gp, u[1, :, block])
            back0 = back0 + dot_nt(gp, u[0, :, block])
        back_send[c] = back1.astype(BF16)
        back_copy(c).start()
        back_own[c] = back0
        return carry

    lax.fori_loop(0, chunks, compute, 0)

    flat = (chunks * rows, width)
    for k, (xk, gk) in enumerate(((x_own, g_own), (x_far, g_far))):
        xs, gs = xk[...].reshape(flat), gk[...].reshape(flat)
        for j in range(expand):
            block = slice(j * width, (j + 1) * width)
            up_grad[k, :, block] = dot_tn(xs, gpre[:, block]).astype(BF16)
            down_grad[k, block, :] = dot_tn(hid[:, block], gs).astype(BF16)
    def drain(c, carry):
        emb_far(c).wait_send()
        pl.when(even)(lambda: acts_far(c).wait_send())
        pl.when(jnp.logical_or(odd_far, beside_late))(lambda: grads_far(c).wait_send())
        pl.when(jnp.logical_not(last))(lambda: acts_near(c).wait_send())
        pl.when(jnp.logical_not(first))(lambda: grads_near(c).wait_send())
        return carry

    lax.fori_loop(0, chunks, drain, 0)

    def finish(c, carry):
        out_copy(c).wait_recv()
        here = pl.ds(pl.multiple_of(c * rows, rows), rows)
        mixed[here] = (out_own[c] + out_got[c].astype(F32)).astype(BF16)
        back_copy(c).wait_recv()
        input_grads[here] = (back_own[c] + back_got[c].astype(F32)).astype(BF16)
        out_copy(c).wait_send()
        back_copy(c).wait_send()
        return carry

    lax.fori_loop(0, chunks, finish, 0)


def flush(*refs):
    done = refs[-1]
    count = done.shape[0]
    copies = [
        pltpu.make_async_copy(refs[i], refs[count + i], done.at[i]) for i in range(count)
    ]
    for copy in copies:
        copy.start()
    for copy in copies:
        copy.wait()


def on_device(acts_prev, embedded, grads_next, loss_grad, up_weight, down_weight):
    sections, tensors = lax.axis_size("section"), lax.axis_size("tensor")
    tokens, width = acts_prev.shape
    up_local, down_local = up_weight[0], down_weight[0]
    factors, _, hidden = up_local.shape
    chunks, rows = CHUNKS, tokens // CHUNKS
    blocks = (chunks, rows, width)
    anywhere = pl.BlockSpec(memory_space=pl.ANY)

    def in_hbm(value):
        return pltpu.with_memory_space_constraint(value, pltpu.HBM)

    shapes = (acts_prev.shape, acts_prev.shape, up_local.shape, down_local.shape)
    results = pl.pallas_call(
        functools.partial(kernel, sections, tensors // 2, hidden // width),
        name="relay_layer",
        out_shape=tuple(pltpu.VMEM(shape, BF16) for shape in shapes),
        in_specs=[anywhere] * 6,
        out_specs=[pl.BlockSpec(memory_space=pltpu.VMEM)] * 4,
        scratch_shapes=[
            pltpu.VMEM(blocks, BF16),
            pltpu.VMEM(blocks, BF16),
            pltpu.VMEM(blocks, BF16),
            pltpu.VMEM(blocks, BF16),
            pltpu.VMEM(up_local.shape, BF16),
            pltpu.VMEM(down_local.shape, BF16),
            pltpu.VMEM((tokens, hidden), BF16),
            pltpu.VMEM((tokens, hidden), BF16),
            pltpu.VMEM(blocks, F32),
            pltpu.VMEM(blocks, F32),
            pltpu.VMEM(blocks, BF16),
            pltpu.VMEM(blocks, BF16),
            pltpu.VMEM(blocks, BF16),
            pltpu.VMEM(blocks, BF16),
            pltpu.SemaphoreType.DMA((7, chunks)),
            pltpu.SemaphoreType.DMA((6, chunks)),
            pltpu.SemaphoreType.DMA((2,)),
            pltpu.SemaphoreType.REGULAR,
            pltpu.SemaphoreType.REGULAR,
        ],
        compiler_params=pltpu.CompilerParams(
            collective_id=0, has_side_effects=True, vmem_limit_bytes=48 << 20
        ),
    )(*map(in_hbm, (acts_prev, embedded, grads_next, loss_grad, up_local, down_local)))
    mixed, input_grads, up_grad, down_grad = pl.pallas_call(
        flush,
        name="flush",
        out_shape=tuple(pltpu.HBM(shape, BF16) for shape in shapes),
        in_specs=[anywhere] * 4,
        out_specs=[anywhere] * 4,
        scratch_shapes=[pltpu.SemaphoreType.DMA((4,))],
        compiler_params=pltpu.CompilerParams(vmem_limit_bytes=1 << 20),
    )(*results)
    return (mixed, input_grads, up_grad[None], down_grad[None])


def solution(mesh):
    in_specs = (
        P("section", "tensor"),
        P(None, "tensor"),
        P("section", "tensor"),
        P(None, "tensor"),
        P("section", None, None, "tensor"),
        P("section", None, "tensor", None),
    )
    out_specs = (
        P("section", "tensor"),
        P("section", "tensor"),
        P("section", None, None, "tensor"),
        P("section", None, "tensor", None),
    )
    return jax.shard_map(
        on_device, mesh=mesh, in_specs=in_specs, out_specs=out_specs, check_vma=False
    )
```

```python
import functools

import jax
import jax.numpy as jnp
from jax import lax
from jax.experimental import pallas as pl
from jax.experimental.pallas import tpu as pltpu
from jax.sharding import PartitionSpec as P

MESH = pl.DeviceIdType.MESH
F32 = jnp.float32
BF16 = jnp.bfloat16
CHUNKS = 2
ROOT = 0.7978845608028654
CUBIC = 0.044715


def dot(a, b):
    return jnp.dot(a, b, preferred_element_type=F32)


def dot_nt(a, b):
    return lax.dot_general(a, b, (((1,), (1,)), ((), ())), preferred_element_type=F32)


def dot_tn(a, b):
    return lax.dot_general(a, b, (((0,), (0,)), ((), ())), preferred_element_type=F32)


def kernel(
    sections, far, expand,
    acts, emb, grads, loss, up, down,
    mixed, input_grads, up_grad, down_grad,
    x_own, x_far, g_own, g_far, u, v, hid, gpre, out_own, back_own,
    out_send, back_send, out_got, back_got,
    send_sem, recv_sem, load_sem, ready, upper_in,
):
    chunks, rows, width = x_own.shape
    section, tensor = lax.axis_index("section"), lax.axis_index("tensor")
    partner = tensor + far - 2 * far * (lax.rem(tensor // far, 2))
    first, last = section == 0, section == sections - 1

    def at(step, place):
        return {"section": section + step, "tensor": place}

    load_u = pltpu.make_async_copy(up, u, load_sem.at[0])
    load_v = pltpu.make_async_copy(down, v, load_sem.at[1])

    corner = jnp.logical_or(tensor == 0, tensor == far)
    late = jnp.logical_and(first, tensor == 0)
    hears_late = jnp.logical_and(
        jnp.logical_and(section <= 1, corner), jnp.logical_not(late)
    )
    barrier = pltpu.get_barrier_semaphore()

    def tell(semaphore, step, place):
        pl.semaphore_signal(
            semaphore, inc=1, device_id=at(step, place), device_id_type=MESH
        )

    even = lax.rem(section, 2) == 0
    odd = jnp.logical_not(even)
    other = 1 - 2 * lax.rem(section, 2)
    has_upper = jnp.logical_and(odd, jnp.logical_not(last))
    has_lower = jnp.logical_and(even, jnp.logical_not(first))

    @pl.when(jnp.logical_not(late))
    def _():
        tell(barrier, 0, partner)
        tell(barrier, other, partner)
        tell(barrier, other, tensor)

        pl.when(has_upper)(lambda: tell(barrier, 1, tensor))

    load_u.start()
    load_v.start()

    def wait_for(peers, when):
        @pl.when(when)
        def _():
            pl.semaphore_wait(barrier, peers)

    wait_for(4, has_lower)
    wait_for(3, jnp.logical_and(jnp.logical_not(has_lower), jnp.logical_not(hears_late)))
    wait_for(2, hears_late)

    @pl.when(late)
    def _():
        tell(ready, 0, partner)
        tell(ready, 1, tensor)

    pl.when(has_lower)(lambda: tell(upper_in, -1, tensor))

    def part(ref, c):
        return ref.at[pl.ds(pl.multiple_of(c * rows, rows), rows)]

    def copy(source, target, c, send, recv, step, place):
        return pltpu.make_async_remote_copy(
            src_ref=source,
            dst_ref=target.at[c],
            send_sem=send_sem.at[send, c],
            recv_sem=recv_sem.at[recv, c],
            device_id=at(step, place),
            device_id_type=MESH,
        )

    def acts_far(c):
        return copy(part(acts, c), x_far, c, 0, 0, 1, partner)

    def grads_far(c):
        return copy(part(grads, c), g_far, c, 1, 1, -1, partner)

    def acts_near(c):
        return copy(part(acts, c), x_own, c, 2, 2, 1, tensor)

    def grads_near(c):
        return copy(part(grads, c), g_own, c, 3, 3, -1, tensor)

    def emb_far(c):
        return copy(part(emb, c), x_far, c, 4, 0, 0, partner)

    def loss_far(c):
        return copy(part(loss, c), g_far, c, 4, 1, 0, partner)

    def pass_acts(c):
        return copy(x_own.at[c], x_far, c, 4, 0, 0, partner)

    def pass_grads(c):
        return copy(g_own.at[c], g_far, c, 4, 1, 0, partner)

    def pass_late(c):
        return copy(g_own.at[c], g_far, c, 1, 1, 0, partner)

    def emb_near(c):
        return pltpu.make_async_copy(part(emb, c), x_own.at[c], recv_sem.at[2, c])

    def loss_near(c):
        return pltpu.make_async_copy(part(loss, c), g_own.at[c], recv_sem.at[3, c])

    def out_copy(c):
        return copy(out_send.at[c], out_got, c, 5, 4, 0, partner)

    def back_copy(c):
        return copy(back_send.at[c], back_got, c, 6, 5, 0, partner)

    def near_late(step, place):
        return jnp.logical_and(section + step == 0, place == 0)

    beside_late, across_late = near_late(0, partner), near_late(-1, partner)
    far_first = jnp.logical_and(first, jnp.logical_not(beside_late))
    odd_far = jnp.logical_and(odd, jnp.logical_not(across_late))
    odd_near = jnp.logical_and(odd, jnp.logical_not(near_late(-1, tensor)))

    def start_far(c, carry):
        pl.when(even)(lambda: acts_far(c).start())
        pl.when(odd_far)(lambda: grads_far(c).start())
        pl.when(far_first)(lambda: emb_far(c).start())
        pl.when(last)(lambda: loss_far(c).start())
        return carry

    def start_near(c, carry):
        pl.when(even)(lambda: acts_near(c).start())
        pl.when(jnp.logical_or(odd_near, has_lower))(lambda: grads_near(c).start())
        pl.when(first)(lambda: emb_near(c).start())
        pl.when(last)(lambda: loss_near(c).start())
        return carry

    def start_upper(c, carry):
        acts_near(c).start()
        return carry

    def start_late(c, carry):
        pl.when(beside_late)(lambda: emb_far(c).start())
        pl.when(near_late(-1, tensor))(lambda: grads_near(c).start())
        return carry

    def pass_on(c, carry):
        acts_near(c).wait_recv()
        grads_near(c).wait_recv()
        pl.when(has_lower)(lambda: pass_acts(c).start())
        pl.when(has_upper)(lambda: pass_grads(c).start())
        pl.when(beside_late)(lambda: pass_late(c).start())
        return carry

    lax.fori_loop(0, chunks, start_near, 0)
    early = jnp.where(has_lower, chunks - 1, chunks)
    lax.fori_loop(0, early, start_far, 0)

    @pl.when(has_upper)
    def _():
        pl.semaphore_wait(upper_in, 1)
        lax.fori_loop(0, chunks, start_upper, 0)

    @pl.when(jnp.logical_and(hears_late, jnp.logical_not(across_late)))
    def _():
        pl.semaphore_wait(ready, 1)
        lax.fori_loop(0, chunks, start_late, 0)

    lax.fori_loop(0, chunks, pass_on, 0)
    lax.fori_loop(early, chunks, start_far, 0)
    load_u.wait()
    load_v.wait()

    def compute(c, carry):
        acts_far(c).wait_recv()
        here = pl.ds(pl.multiple_of(c * rows, rows), rows)
        xo, xf = x_own[c], x_far[c]
        slopes = []
        out0 = xo.astype(F32)
        out1 = jnp.zeros((rows, width), F32)
        for j in range(expand):
            block = slice(j * width, (j + 1) * width)
            pre = dot(xo, u[0, :, block]) + dot(xf, u[1, :, block])
            square = pre * pre
            t = jnp.tanh(ROOT * (pre + CUBIC * (square * pre)))
            half = 0.5 * (1.0 + t)
            slopes.append(
                half + 0.5 * pre * (1.0 - t * t) * (ROOT * (1.0 + 3.0 * CUBIC * square))
            )
            h = (pre * half).astype(BF16)
            hid[here, block] = h
            out1 = out1 + dot(h, v[1, block, :])
            out0 = out0 + dot(h, v[0, block, :])
        out_send[c] = out1.astype(BF16)
        out_copy(c).start()
        out_own[c] = out0
        grads_far(c).wait_recv()
        go, gf = g_own[c], g_far[c]
        back0 = go.astype(F32)
        back1 = jnp.zeros((rows, width), F32)
        for j in range(expand):
            block = slice(j * width, (j + 1) * width)
            gh = dot_nt(go, v[0, block, :]) + dot_nt(gf, v[1, block, :])
            gp = (gh * slopes[j]).astype(BF16)
            gpre[here, block] = gp
            back1 = back1 + dot_nt(gp, u[1, :, block])
            back0 = back0 + dot_nt(gp, u[0, :, block])
        back_send[c] = back1.astype(BF16)
        back_copy(c).start()
        back_own[c] = back0
        return carry

    lax.fori_loop(0, chunks, compute, 0)

    flat = (chunks * rows, width)
    for k, (xk, gk) in enumerate(((x_own, g_own), (x_far, g_far))):
        xs, gs = xk[...].reshape(flat), gk[...].reshape(flat)
        for j in range(expand):
            block = slice(j * width, (j + 1) * width)
            up_grad[k, :, block] = dot_tn(xs, gpre[:, block]).astype(BF16)
            down_grad[k, block, :] = dot_tn(hid[:, block], gs).astype(BF16)

    def drain(c, carry):
        emb_far(c).wait_send()
        pl.when(even)(lambda: acts_far(c).wait_send())
        pl.when(jnp.logical_or(odd_far, beside_late))(lambda: grads_far(c).wait_send())
        pl.when(jnp.logical_not(last))(lambda: acts_near(c).wait_send())
        pl.when(jnp.logical_not(first))(lambda: grads_near(c).wait_send())
        return carry

    lax.fori_loop(0, chunks, drain, 0)

    def finish(c, carry):
        out_copy(c).wait_recv()
        here = pl.ds(pl.multiple_of(c * rows, rows), rows)
        mixed[here] = (out_own[c] + out_got[c].astype(F32)).astype(BF16)
        back_copy(c).wait_recv()
        input_grads[here] = (back_own[c] + back_got[c].astype(F32)).astype(BF16)
        out_copy(c).wait_send()
        back_copy(c).wait_send()
        return carry

    lax.fori_loop(0, chunks, finish, 0)


def flush(*refs):
    done = refs[-1]
    count = done.shape[0]
    copies = [
        pltpu.make_async_copy(refs[i], refs[count + i], done.at[i]) for i in range(count)
    ]
    for copy in copies:
        copy.start()
    for copy in copies:
        copy.wait()


def on_device(acts_prev, embedded, grads_next, loss_grad, up_weight, down_weight):
    sections, tensors = lax.axis_size("section"), lax.axis_size("tensor")
    tokens, width = acts_prev.shape
    up_local, down_local = up_weight[0], down_weight[0]
    factors, _, hidden = up_local.shape
    chunks, rows = CHUNKS, tokens // CHUNKS
    blocks = (chunks, rows, width)
    anywhere = pl.BlockSpec(memory_space=pl.ANY)

    def in_hbm(value):
        return pltpu.with_memory_space_constraint(value, pltpu.HBM)

    shapes = (acts_prev.shape, acts_prev.shape, up_local.shape, down_local.shape)
    results = pl.pallas_call(
        functools.partial(kernel, sections, tensors // 2, hidden // width),
        name="relay_layer",
        out_shape=tuple(pltpu.VMEM(shape, BF16) for shape in shapes),
        in_specs=[anywhere] * 6,
        out_specs=[pl.BlockSpec(memory_space=pltpu.VMEM)] * 4,
        scratch_shapes=[
            pltpu.VMEM(blocks, BF16),
            pltpu.VMEM(blocks, BF16),
            pltpu.VMEM(blocks, BF16),
            pltpu.VMEM(blocks, BF16),
            pltpu.VMEM(up_local.shape, BF16),
            pltpu.VMEM(down_local.shape, BF16),
            pltpu.VMEM((tokens, hidden), BF16),
            pltpu.VMEM((tokens, hidden), BF16),
            pltpu.VMEM(blocks, F32),
            pltpu.VMEM(blocks, F32),
            pltpu.VMEM(blocks, BF16),
            pltpu.VMEM(blocks, BF16),
            pltpu.VMEM(blocks, BF16),
            pltpu.VMEM(blocks, BF16),
            pltpu.SemaphoreType.DMA((7, chunks)),
            pltpu.SemaphoreType.DMA((6, chunks)),
            pltpu.SemaphoreType.DMA((2,)),
            pltpu.SemaphoreType.REGULAR,
            pltpu.SemaphoreType.REGULAR,
        ],
        compiler_params=pltpu.CompilerParams(
            collective_id=0, has_side_effects=True, vmem_limit_bytes=48 << 20
        ),
    )(*map(in_hbm, (acts_prev, embedded, grads_next, loss_grad, up_local, down_local)))
    mixed, input_grads, up_grad, down_grad = pl.pallas_call(
        flush,
        name="flush",
        out_shape=tuple(pltpu.HBM(shape, BF16) for shape in shapes),
        in_specs=[anywhere] * 4,
        out_specs=[anywhere] * 4,
        scratch_shapes=[pltpu.SemaphoreType.DMA((4,))],
        compiler_params=pltpu.CompilerParams(vmem_limit_bytes=1 << 20),
    )(*results)
    return (mixed, input_grads, up_grad[None], down_grad[None])


def solution(mesh):
    in_specs = (
        P("section", "tensor"),
        P(None, "tensor"),
        P("section", "tensor"),
        P(None, "tensor"),
        P("section", None, None, "tensor"),
        P("section", None, "tensor", None),
    )
    out_specs = (
        P("section", "tensor"),
        P("section", "tensor"),
        P("section", None, None, "tensor"),
        P("section", None, "tensor", None),
    )
    return jax.shard_map(
        on_device, mesh=mesh, in_specs=in_specs, out_specs=out_specs, check_vma=False
    )
```

```python
import functools

import jax
import jax.numpy as jnp
from jax import lax
from jax.experimental import pallas as pl
from jax.experimental.pallas import tpu as pltpu
from jax.sharding import PartitionSpec as P

MESH = pl.DeviceIdType.MESH
F32 = jnp.float32
BF16 = jnp.bfloat16
CHUNKS = 2
ROOT = 0.7978845608028654
CUBIC = 0.044715


def dot(a, b):
    return jnp.dot(a, b, preferred_element_type=F32)


def dot_nt(a, b):
    return lax.dot_general(a, b, (((1,), (1,)), ((), ())), preferred_element_type=F32)


def dot_tn(a, b):
    return lax.dot_general(a, b, (((0,), (0,)), ((), ())), preferred_element_type=F32)


def kernel(
    sections, far, expand,
    acts, emb, grads, loss, up, down,
    mixed, input_grads, up_grad, down_grad,
    x_own, x_far, g_own, g_far, u, v, hid, gpre, out_own, back_own,
    out_send, back_send, out_got, back_got,
    send_sem, recv_sem, load_sem, ready, upper_in,
):
    chunks, rows, width = x_own.shape
    section, tensor = lax.axis_index("section"), lax.axis_index("tensor")
    partner = tensor + far - 2 * far * (lax.rem(tensor // far, 2))
    first, last = section == 0, section == sections - 1

    def at(step, place):
        return {"section": section + step, "tensor": place}

    load_u = pltpu.make_async_copy(up, u, load_sem.at[0])
    load_v = pltpu.make_async_copy(down, v, load_sem.at[1])

    corner = jnp.logical_or(tensor == 0, tensor == far)
    late = jnp.logical_and(first, tensor == 0)
    hears_late = jnp.logical_and(
        jnp.logical_and(section <= 1, corner), jnp.logical_not(late)
    )
    barrier = pltpu.get_barrier_semaphore()

    def tell(semaphore, step, place):
        pl.semaphore_signal(
            semaphore, inc=1, device_id=at(step, place), device_id_type=MESH
        )

    even = lax.rem(section, 2) == 0
    odd = jnp.logical_not(even)
    other = 1 - 2 * lax.rem(section, 2)
    has_upper = jnp.logical_and(odd, jnp.logical_not(last))
    has_lower = jnp.logical_and(even, jnp.logical_not(first))

    @pl.when(jnp.logical_not(late))
    def _():
        tell(barrier, 0, partner)
        tell(barrier, other, partner)
        tell(barrier, other, tensor)

        pl.when(has_upper)(lambda: tell(barrier, 1, tensor))

    load_u.start()
    load_v.start()

    def wait_for(peers, when):
        @pl.when(when)
        def _():
            pl.semaphore_wait(barrier, peers)

    wait_for(4, has_lower)
    wait_for(3, jnp.logical_and(jnp.logical_not(has_lower), jnp.logical_not(hears_late)))
    wait_for(2, hears_late)

    @pl.when(late)
    def _():
        tell(ready, 0, partner)
        tell(ready, 1, tensor)

    pl.when(has_lower)(lambda: tell(upper_in, -1, tensor))

    def part(ref, c):
        return ref.at[pl.ds(pl.multiple_of(c * rows, rows), rows)]

    def copy(source, target, c, send, recv, step, place):
        return pltpu.make_async_remote_copy(
            src_ref=source,
            dst_ref=target.at[c],
            send_sem=send_sem.at[send, c],
            recv_sem=recv_sem.at[recv, c],
            device_id=at(step, place),
            device_id_type=MESH,
        )

    def acts_far(c):
        return copy(part(acts, c), x_far, c, 0, 0, 1, partner)

    def grads_far(c):
        return copy(part(grads, c), g_far, c, 1, 1, -1, partner)

    def acts_near(c):
        return copy(part(acts, c), x_own, c, 2, 2, 1, tensor)

    def grads_near(c):
        return copy(part(grads, c), g_own, c, 3, 3, -1, tensor)

    def emb_far(c):
        return copy(part(emb, c), x_far, c, 4, 0, 0, partner)

    def loss_far(c):
        return copy(part(loss, c), g_far, c, 4, 1, 0, partner)

    def pass_acts(c):
        return copy(x_own.at[c], x_far, c, 4, 0, 0, partner)

    def pass_grads(c):
        return copy(g_own.at[c], g_far, c, 4, 1, 0, partner)

    def pass_late(c):
        return copy(g_own.at[c], g_far, c, 1, 1, 0, partner)

    def wait_for_block(target, recv, c):
        copy(target.at[c], target, c, 0, recv, 0, partner).wait_recv()

    def emb_near(c):
        return pltpu.make_async_copy(part(emb, c), x_own.at[c], recv_sem.at[2, c])

    def loss_near(c):
        return pltpu.make_async_copy(part(loss, c), g_own.at[c], recv_sem.at[3, c])

    def out_copy(c):
        return copy(out_send.at[c], out_got, c, 5, 4, 0, partner)

    def back_copy(c):
        return copy(back_send.at[c], back_got, c, 6, 5, 0, partner)

    def near_late(step, place):
        return jnp.logical_and(section + step == 0, place == 0)

    beside_late, across_late = near_late(0, partner), near_late(-1, partner)
    far_first = jnp.logical_and(first, jnp.logical_not(beside_late))
    odd_far = jnp.logical_and(odd, jnp.logical_not(across_late))
    odd_near = jnp.logical_and(odd, jnp.logical_not(near_late(-1, tensor)))

    def start_far(c, carry):
        pl.when(even)(lambda: acts_far(c).start())
        pl.when(odd_far)(lambda: grads_far(c).start())
        pl.when(far_first)(lambda: emb_far(c).start())
        pl.when(last)(lambda: loss_far(c).start())
        return carry

    def start_near(c, carry):
        pl.when(even)(lambda: acts_near(c).start())
        pl.when(jnp.logical_or(odd_near, has_lower))(lambda: grads_near(c).start())
        pl.when(first)(lambda: emb_near(c).start())
        pl.when(last)(lambda: loss_near(c).start())
        return carry

    def start_upper(c, carry):
        acts_near(c).start()
        return carry

    def start_late(c, carry):
        pl.when(beside_late)(lambda: emb_far(c).start())
        pl.when(near_late(-1, tensor))(lambda: grads_near(c).start())
        return carry

    def pass_on(c, carry):
        wait_for_block(x_own, 2, c)
        wait_for_block(g_own, 3, c)
        pl.when(has_lower)(lambda: pass_acts(c).start())
        pl.when(has_upper)(lambda: pass_grads(c).start())
        pl.when(beside_late)(lambda: pass_late(c).start())
        return carry

    lax.fori_loop(0, chunks, start_near, 0)
    early = jnp.where(has_lower, chunks - 1, chunks)
    lax.fori_loop(0, early, start_far, 0)

    @pl.when(has_upper)
    def _():
        pl.semaphore_wait(upper_in, 1)
        lax.fori_loop(0, chunks, start_upper, 0)

    @pl.when(jnp.logical_and(hears_late, jnp.logical_not(across_late)))
    def _():
        pl.semaphore_wait(ready, 1)
        lax.fori_loop(0, chunks, start_late, 0)

    lax.fori_loop(0, chunks, pass_on, 0)
    lax.fori_loop(early, chunks, start_far, 0)
    load_u.wait()
    load_v.wait()

    def compute(c, carry):
        wait_for_block(x_far, 0, c)
        here = pl.ds(pl.multiple_of(c * rows, rows), rows)
        xo, xf = x_own[c], x_far[c]
        slopes = []
        out0 = xo.astype(F32)
        out1 = jnp.zeros((rows, width), F32)
        for j in range(expand):
            block = slice(j * width, (j + 1) * width)
            pre = dot(xo, u[0, :, block]) + dot(xf, u[1, :, block])
            square = pre * pre
            t = jnp.tanh(ROOT * (pre + CUBIC * (square * pre)))
            half = 0.5 * (1.0 + t)
            slopes.append(
                half + 0.5 * pre * (1.0 - t * t) * (ROOT * (1.0 + 3.0 * CUBIC * square))
            )
            h = (pre * half).astype(BF16)
            hid[here, block] = h
            out1 = out1 + dot(h, v[1, block, :])
            out0 = out0 + dot(h, v[0, block, :])
        out_send[c] = out1.astype(BF16)
        out_copy(c).start()
        out_own[c] = out0
        wait_for_block(g_far, 1, c)
        go, gf = g_own[c], g_far[c]
        back0 = go.astype(F32)
        back1 = jnp.zeros((rows, width), F32)
        for j in range(expand):
            block = slice(j * width, (j + 1) * width)
            gh = dot_nt(go, v[0, block, :]) + dot_nt(gf, v[1, block, :])
            gp = (gh * slopes[j]).astype(BF16)
            gpre[here, block] = gp
            back1 = back1 + dot_nt(gp, u[1, :, block])
            back0 = back0 + dot_nt(gp, u[0, :, block])
        back_send[c] = back1.astype(BF16)
        back_copy(c).start()
        back_own[c] = back0
        return carry

    lax.fori_loop(0, chunks, compute, 0)

    flat = (chunks * rows, width)
    for k, (xk, gk) in enumerate(((x_own, g_own), (x_far, g_far))):
        xs, gs = xk[...].reshape(flat), gk[...].reshape(flat)
        for j in range(expand):
            block = slice(j * width, (j + 1) * width)
            up_grad[k, :, block] = dot_tn(xs, gpre[:, block]).astype(BF16)
            down_grad[k, block, :] = dot_tn(hid[:, block], gs).astype(BF16)

    def drain(c, carry):
        emb_far(c).wait_send()
        pl.when(even)(lambda: acts_far(c).wait_send())
        pl.when(odd_far)(lambda: grads_far(c).wait_send())
        pl.when(beside_late)(lambda: pass_late(c).wait_send())
        pl.when(jnp.logical_not(last))(lambda: acts_near(c).wait_send())
        pl.when(jnp.logical_not(first))(lambda: grads_near(c).wait_send())
        return carry

    lax.fori_loop(0, chunks, drain, 0)

    def finish(c, carry):
        out_copy(c).wait_recv()
        here = pl.ds(pl.multiple_of(c * rows, rows), rows)
        mixed[here] = (out_own[c] + out_got[c].astype(F32)).astype(BF16)
        back_copy(c).wait_recv()
        input_grads[here] = (back_own[c] + back_got[c].astype(F32)).astype(BF16)
        out_copy(c).wait_send()
        back_copy(c).wait_send()
        return carry

    lax.fori_loop(0, chunks, finish, 0)


def flush(*refs):
    done = refs[-1]
    count = done.shape[0]
    copies = [
        pltpu.make_async_copy(refs[i], refs[count + i], done.at[i]) for i in range(count)
    ]
    for copy in copies:
        copy.start()
    for copy in copies:
        copy.wait()


def on_device(acts_prev, embedded, grads_next, loss_grad, up_weight, down_weight):
    sections, tensors = lax.axis_size("section"), lax.axis_size("tensor")
    tokens, width = acts_prev.shape
    up_local, down_local = up_weight[0], down_weight[0]
    factors, _, hidden = up_local.shape
    chunks, rows = CHUNKS, tokens // CHUNKS
    blocks = (chunks, rows, width)
    anywhere = pl.BlockSpec(memory_space=pl.ANY)

    def in_hbm(value):
        return pltpu.with_memory_space_constraint(value, pltpu.HBM)

    shapes = (acts_prev.shape, acts_prev.shape, up_local.shape, down_local.shape)
    results = pl.pallas_call(
        functools.partial(kernel, sections, tensors // 2, hidden // width),
        name="relay_layer",
        out_shape=tuple(pltpu.VMEM(shape, BF16) for shape in shapes),
        in_specs=[anywhere] * 6,
        out_specs=[pl.BlockSpec(memory_space=pltpu.VMEM)] * 4,
        scratch_shapes=[
            pltpu.VMEM(blocks, BF16),
            pltpu.VMEM(blocks, BF16),
            pltpu.VMEM(blocks, BF16),
            pltpu.VMEM(blocks, BF16),
            pltpu.VMEM(up_local.shape, BF16),
            pltpu.VMEM(down_local.shape, BF16),
            pltpu.VMEM((tokens, hidden), BF16),
            pltpu.VMEM((tokens, hidden), BF16),
            pltpu.VMEM(blocks, F32),
            pltpu.VMEM(blocks, F32),
            pltpu.VMEM(blocks, BF16),
            pltpu.VMEM(blocks, BF16),
            pltpu.VMEM(blocks, BF16),
            pltpu.VMEM(blocks, BF16),
            pltpu.SemaphoreType.DMA((7, chunks)),
            pltpu.SemaphoreType.DMA((6, chunks)),
            pltpu.SemaphoreType.DMA((2,)),
            pltpu.SemaphoreType.REGULAR,
            pltpu.SemaphoreType.REGULAR,
        ],
        compiler_params=pltpu.CompilerParams(
            collective_id=0, has_side_effects=True, vmem_limit_bytes=48 << 20
        ),
    )(*map(in_hbm, (acts_prev, embedded, grads_next, loss_grad, up_local, down_local)))
    mixed, input_grads, up_grad, down_grad = pl.pallas_call(
        flush,
        name="flush",
        out_shape=tuple(pltpu.HBM(shape, BF16) for shape in shapes),
        in_specs=[anywhere] * 4,
        out_specs=[anywhere] * 4,
        scratch_shapes=[pltpu.SemaphoreType.DMA((4,))],
        compiler_params=pltpu.CompilerParams(vmem_limit_bytes=1 << 20),
    )(*results)
    return (mixed, input_grads, up_grad[None], down_grad[None])


def solution(mesh):
    in_specs = (
        P("section", "tensor"),
        P(None, "tensor"),
        P("section", "tensor"),
        P(None, "tensor"),
        P("section", None, None, "tensor"),
        P("section", None, "tensor", None),
    )
    out_specs = (
        P("section", "tensor"),
        P("section", "tensor"),
        P("section", None, None, "tensor"),
        P("section", None, "tensor", None),
    )
    return jax.shard_map(
        on_device, mesh=mesh, in_specs=in_specs, out_specs=out_specs, check_vma=False
    )
```

```python
import functools

import jax
import jax.numpy as jnp
from jax import lax
from jax.experimental import pallas as pl
from jax.experimental.pallas import tpu as pltpu
from jax.sharding import PartitionSpec as P

MESH = pl.DeviceIdType.MESH
F32 = jnp.float32
BF16 = jnp.bfloat16
CHUNKS = 2
ROOT = 0.7978845608028654
CUBIC = 0.044715


def dot(a, b):
    return jnp.dot(a, b, preferred_element_type=F32)


def dot_nt(a, b):
    return lax.dot_general(a, b, (((1,), (1,)), ((), ())), preferred_element_type=F32)


def dot_tn(a, b):
    return lax.dot_general(a, b, (((0,), (0,)), ((), ())), preferred_element_type=F32)


def kernel(
    sections, far, expand,
    acts, emb, grads, loss, up, down,
    mixed, input_grads, up_grad, down_grad,
    x_own, x_far, g_own, g_far, u, v, hid, gpre, out_own, back_own,
    out_send, back_send, out_got, back_got,
    send_sem, recv_sem, load_sem, ready, upper_in,
):
    chunks, rows, width = x_own.shape
    section, tensor = lax.axis_index("section"), lax.axis_index("tensor")
    partner = tensor + far - 2 * far * (lax.rem(tensor // far, 2))
    first, last = section == 0, section == sections - 1

    def at(step, place):
        return {"section": section + step, "tensor": place}

    load_u = pltpu.make_async_copy(up, u, load_sem.at[0])
    load_v = pltpu.make_async_copy(down, v, load_sem.at[1])

    corner = jnp.logical_or(tensor == 0, tensor == far)
    late = jnp.logical_and(first, tensor == 0)
    hears_late = jnp.logical_and(
        jnp.logical_and(section <= 1, corner), jnp.logical_not(late)
    )
    barrier = pltpu.get_barrier_semaphore()

    def tell(semaphore, step, place):
        pl.semaphore_signal(
            semaphore, inc=1, device_id=at(step, place), device_id_type=MESH
        )

    even = lax.rem(section, 2) == 0
    odd = jnp.logical_not(even)
    other = 1 - 2 * lax.rem(section, 2)
    has_upper = jnp.logical_and(odd, jnp.logical_not(last))
    has_lower = jnp.logical_and(even, jnp.logical_not(first))

    @pl.when(jnp.logical_not(late))
    def _():
        tell(barrier, 0, partner)
        tell(barrier, other, partner)
        tell(barrier, other, tensor)

        pl.when(has_upper)(lambda: tell(barrier, 1, tensor))

    load_u.start()
    load_v.start()

    def wait_for(peers, when):
        @pl.when(when)
        def _():
            pl.semaphore_wait(barrier, peers)

    wait_for(4, has_lower)
    wait_for(3, jnp.logical_and(jnp.logical_not(has_lower), jnp.logical_not(hears_late)))
    wait_for(2, hears_late)

    @pl.when(late)
    def _():
        tell(ready, 0, partner)
        tell(ready, 1, tensor)

    pl.when(has_lower)(lambda: tell(upper_in, -1, tensor))

    def part(ref, c):
        return ref.at[pl.ds(pl.multiple_of(c * rows, rows), rows)]

    def copy(source, target, c, send, recv, step, place):
        return pltpu.make_async_remote_copy(
            src_ref=source,
            dst_ref=target.at[c],
            send_sem=send_sem.at[send, c],
            recv_sem=recv_sem.at[recv, c],
            device_id=at(step, place),
            device_id_type=MESH,
        )

    def acts_far(c):
        return copy(part(acts, c), x_far, c, 0, 0, 1, partner)

    def grads_far(c):
        return copy(part(grads, c), g_far, c, 1, 1, -1, partner)

    def acts_near(c):
        return copy(part(acts, c), x_own, c, 2, 2, 1, tensor)

    def grads_near(c):
        return copy(part(grads, c), g_own, c, 3, 3, -1, tensor)

    def emb_far(c):
        return copy(part(emb, c), x_far, c, 4, 0, 0, partner)

    def loss_far(c):
        return copy(part(loss, c), g_far, c, 4, 1, 0, partner)

    def pass_acts(c):
        return copy(x_own.at[c], x_far, c, 4, 0, 0, partner)

    def pass_grads(c):
        return copy(g_own.at[c], g_far, c, 4, 1, 0, partner)

    def pass_late(c):
        return copy(g_own.at[c], g_far, c, 1, 1, 0, partner)

    def wait_for_block(target, recv, c):
        copy(target.at[c], target, c, 0, recv, 0, partner).wait_recv()

    def emb_near(c):
        return pltpu.make_async_copy(part(emb, c), x_own.at[c], recv_sem.at[2, c])

    def loss_near(c):
        return pltpu.make_async_copy(part(loss, c), g_own.at[c], recv_sem.at[3, c])

    def out_copy(c):
        return copy(out_send.at[c], out_got, c, 5, 4, 0, partner)

    def back_copy(c):
        return copy(back_send.at[c], back_got, c, 6, 5, 0, partner)

    def near_late(step, place):
        return jnp.logical_and(section + step == 0, place == 0)

    beside_late, across_late = near_late(0, partner), near_late(-1, partner)
    far_first = jnp.logical_and(first, jnp.logical_not(beside_late))
    odd_far = jnp.logical_and(odd, jnp.logical_not(across_late))
    odd_near = jnp.logical_and(odd, jnp.logical_not(near_late(-1, tensor)))

    def start_far(c, carry):
        pl.when(even)(lambda: acts_far(c).start())
        pl.when(odd_far)(lambda: grads_far(c).start())
        pl.when(far_first)(lambda: emb_far(c).start())
        pl.when(last)(lambda: loss_far(c).start())
        return carry

    def start_near(c, carry):
        pl.when(even)(lambda: acts_near(c).start())
        pl.when(jnp.logical_or(odd_near, has_lower))(lambda: grads_near(c).start())
        pl.when(first)(lambda: emb_near(c).start())
        pl.when(last)(lambda: loss_near(c).start())
        return carry

    def start_upper(c, carry):
        acts_near(c).start()
        return carry

    def start_late(c, carry):
        pl.when(beside_late)(lambda: emb_far(c).start())
        pl.when(near_late(-1, tensor))(lambda: grads_near(c).start())
        return carry

    def pass_on(c, carry):
        wait_for_block(x_own, 2, c)
        wait_for_block(g_own, 3, c)
        pl.when(has_lower)(lambda: pass_acts(c).start())
        pl.when(has_upper)(lambda: pass_grads(c).start())
        pl.when(beside_late)(lambda: pass_late(c).start())
        return carry

    early = jnp.where(has_lower, chunks - 1, chunks)
    lax.fori_loop(0, early, start_far, 0)
    lax.fori_loop(0, chunks, start_near, 0)

    @pl.when(has_upper)
    def _():
        pl.semaphore_wait(upper_in, 1)
        lax.fori_loop(0, chunks, start_upper, 0)

    @pl.when(jnp.logical_and(hears_late, jnp.logical_not(across_late)))
    def _():
        pl.semaphore_wait(ready, 1)
        lax.fori_loop(0, chunks, start_late, 0)

    lax.fori_loop(0, chunks, pass_on, 0)
    lax.fori_loop(early, chunks, start_far, 0)
    load_u.wait()
    load_v.wait()

    def compute(c, carry):
        wait_for_block(x_far, 0, c)
        here = pl.ds(pl.multiple_of(c * rows, rows), rows)
        xo, xf = x_own[c], x_far[c]
        slopes = []
        out0 = xo.astype(F32)
        out1 = jnp.zeros((rows, width), F32)
        for j in range(expand):
            block = slice(j * width, (j + 1) * width)
            pre = dot(xo, u[0, :, block]) + dot(xf, u[1, :, block])
            square = pre * pre
            t = jnp.tanh(ROOT * (pre + CUBIC * (square * pre)))
            half = 0.5 * (1.0 + t)
            slopes.append(
                half + 0.5 * pre * (1.0 - t * t) * (ROOT * (1.0 + 3.0 * CUBIC * square))
            )
            h = (pre * half).astype(BF16)
            hid[here, block] = h
            out1 = out1 + dot(h, v[1, block, :])
            out0 = out0 + dot(h, v[0, block, :])
        out_send[c] = out1.astype(BF16)
        out_copy(c).start()
        out_own[c] = out0
        wait_for_block(g_far, 1, c)
        go, gf = g_own[c], g_far[c]
        back0 = go.astype(F32)
        back1 = jnp.zeros((rows, width), F32)
        for j in range(expand):
            block = slice(j * width, (j + 1) * width)
            gh = dot_nt(go, v[0, block, :]) + dot_nt(gf, v[1, block, :])
            gp = (gh * slopes[j]).astype(BF16)
            gpre[here, block] = gp
            back1 = back1 + dot_nt(gp, u[1, :, block])
            back0 = back0 + dot_nt(gp, u[0, :, block])
        back_send[c] = back1.astype(BF16)
        back_copy(c).start()
        back_own[c] = back0
        return carry

    lax.fori_loop(0, chunks, compute, 0)

    flat = (chunks * rows, width)
    for k, (xk, gk) in enumerate(((x_own, g_own), (x_far, g_far))):
        xs, gs = xk[...].reshape(flat), gk[...].reshape(flat)
        for j in range(expand):
            block = slice(j * width, (j + 1) * width)
            up_grad[k, :, block] = dot_tn(xs, gpre[:, block]).astype(BF16)
            down_grad[k, block, :] = dot_tn(hid[:, block], gs).astype(BF16)

    def drain(c, carry):
        emb_far(c).wait_send()
        pl.when(even)(lambda: acts_far(c).wait_send())
        pl.when(odd_far)(lambda: grads_far(c).wait_send())
        pl.when(beside_late)(lambda: pass_late(c).wait_send())
        pl.when(jnp.logical_not(last))(lambda: acts_near(c).wait_send())
        pl.when(jnp.logical_not(first))(lambda: grads_near(c).wait_send())
        return carry

    lax.fori_loop(0, chunks, drain, 0)

    def finish(c, carry):
        out_copy(c).wait_recv()
        here = pl.ds(pl.multiple_of(c * rows, rows), rows)
        mixed[here] = (out_own[c] + out_got[c].astype(F32)).astype(BF16)
        back_copy(c).wait_recv()
        input_grads[here] = (back_own[c] + back_got[c].astype(F32)).astype(BF16)
        out_copy(c).wait_send()
        back_copy(c).wait_send()
        return carry

    lax.fori_loop(0, chunks, finish, 0)


def flush(*refs):
    done = refs[-1]
    count = done.shape[0]
    copies = [
        pltpu.make_async_copy(refs[i], refs[count + i], done.at[i]) for i in range(count)
    ]
    for copy in copies:
        copy.start()
    for copy in copies:
        copy.wait()


def on_device(acts_prev, embedded, grads_next, loss_grad, up_weight, down_weight):
    sections, tensors = lax.axis_size("section"), lax.axis_size("tensor")
    tokens, width = acts_prev.shape
    up_local, down_local = up_weight[0], down_weight[0]
    factors, _, hidden = up_local.shape
    chunks, rows = CHUNKS, tokens // CHUNKS
    blocks = (chunks, rows, width)
    anywhere = pl.BlockSpec(memory_space=pl.ANY)

    def in_hbm(value):
        return pltpu.with_memory_space_constraint(value, pltpu.HBM)

    shapes = (acts_prev.shape, acts_prev.shape, up_local.shape, down_local.shape)
    results = pl.pallas_call(
        functools.partial(kernel, sections, tensors // 2, hidden // width),
        name="relay_layer",
        out_shape=tuple(pltpu.VMEM(shape, BF16) for shape in shapes),
        in_specs=[anywhere] * 6,
        out_specs=[pl.BlockSpec(memory_space=pltpu.VMEM)] * 4,
        scratch_shapes=[
            pltpu.VMEM(blocks, BF16),
            pltpu.VMEM(blocks, BF16),
            pltpu.VMEM(blocks, BF16),
            pltpu.VMEM(blocks, BF16),
            pltpu.VMEM(up_local.shape, BF16),
            pltpu.VMEM(down_local.shape, BF16),
            pltpu.VMEM((tokens, hidden), BF16),
            pltpu.VMEM((tokens, hidden), BF16),
            pltpu.VMEM(blocks, F32),
            pltpu.VMEM(blocks, F32),
            pltpu.VMEM(blocks, BF16),
            pltpu.VMEM(blocks, BF16),
            pltpu.VMEM(blocks, BF16),
            pltpu.VMEM(blocks, BF16),
            pltpu.SemaphoreType.DMA((7, chunks)),
            pltpu.SemaphoreType.DMA((6, chunks)),
            pltpu.SemaphoreType.DMA((2,)),
            pltpu.SemaphoreType.REGULAR,
            pltpu.SemaphoreType.REGULAR,
        ],
        compiler_params=pltpu.CompilerParams(
            collective_id=0, has_side_effects=True, vmem_limit_bytes=48 << 20
        ),
    )(*map(in_hbm, (acts_prev, embedded, grads_next, loss_grad, up_local, down_local)))
    mixed, input_grads, up_grad, down_grad = pl.pallas_call(
        flush,
        name="flush",
        out_shape=tuple(pltpu.HBM(shape, BF16) for shape in shapes),
        in_specs=[anywhere] * 4,
        out_specs=[anywhere] * 4,
        scratch_shapes=[pltpu.SemaphoreType.DMA((4,))],
        compiler_params=pltpu.CompilerParams(vmem_limit_bytes=1 << 20),
    )(*results)
    return (mixed, input_grads, up_grad[None], down_grad[None])


def solution(mesh):
    in_specs = (
        P("section", "tensor"),
        P(None, "tensor"),
        P("section", "tensor"),
        P(None, "tensor"),
        P("section", None, None, "tensor"),
        P("section", None, "tensor", None),
    )
    out_specs = (
        P("section", "tensor"),
        P("section", "tensor"),
        P("section", None, None, "tensor"),
        P("section", None, "tensor", None),
    )
    return jax.shard_map(
        on_device, mesh=mesh, in_specs=in_specs, out_specs=out_specs, check_vma=False
    )
```
